32 devices in a mesh: tenant: 8 (over z, x), tp: 4 (over y, core).
Axes of the slice: x: 2, y: 2, z: 4, core: 2. Of those that a mesh axis runs over, the one named last changes fastest.
Arguments:
- src_tokens: bfloat16 [96, 64, 1024], P('tenant'), may hold values from -64 to 64
- pair_tenant: int32 [96], P('tenant'), may hold values from 0 to 7, as said below
- pair_length: int32 [96], P('tenant'), may hold values from 1 to 64
- norm_gain: float32 [8, 1024], P('tenant'), may hold values from 0.1 to 1.9
- w_query: bfloat16 [8, 1024, 4096], P('tenant', None, 'tp'), may hold values from -1 to 1
- w_key: bfloat16 [8, 1024, 4096], P('tenant', None, 'tp'), may hold values from -1 to 1
- w_value: bfloat16 [8, 1024, 4096], P('tenant', None, 'tp'), may hold values from -0.1875 to 0.1875
- w_out: bfloat16 [8, 4096, 1024], P('tenant', 'tp'), may hold values from -0.09375 to 0.09375
- rel_bias: float32 [8, 32, 32], P('tenant', None, 'tp'), may hold values from -6 to 6
Outputs:
- layer_out: bfloat16 [4096, 1024], P(('tenant', 'tp'))
The draws below stay inside these ranges and needn't reach their ends.
Inputs may be any that keep to these rules, and one draw needn't show every extreme that they name: `pair_tenant`: the pairs of one retriever shard bound for one tenant have pair_length summing to at most 64; in every draw some tenant receives exactly 64 tokens from every shard.
All inputs are finite; a program needn't handle non-finite values.
Results may differ from the reference program's by a relative error of at most 0.0065.
Values may be sent and summed in bfloat16 or wider, within the bound.
No kernel may reach another device: no remote copies, remote signals or barrier semaphores. Data moves between devices by JAX's collectives and lax.ppermute only.
A program may use at most 128 MiB of HBM per device.

```python
import math
import jax
import jax.numpy as jnp
import numpy as np
from jax import lax

D = 1024
HEADS = 32
DK = 128
BUCKETS = 32
CAP = 64
SHARD_PAIRS = 12
PAIRS_ALL = 96
ROWS = 4096
N_TENANT = 8
N_TP = 4


def routing(key):
    mixed_key = jax.random.fold_in(key, 17)
    favored_key, tenant_key, length_key, pick_key = jax.random.split(mixed_key, 4)
    shard_count = PAIRS_ALL // SHARD_PAIRS
    favored = jax.random.randint(favored_key, (), 0, shard_count)
    picked = jax.random.randint(pick_key, (shard_count, 1), 0, SHARD_PAIRS)
    is_picked = jnp.arange(SHARD_PAIRS)[None, :] == picked
    tenant_grid = jax.random.randint(tenant_key, (shard_count, SHARD_PAIRS), 0, shard_count)
    tenant_grid = jnp.where(is_picked, favored, tenant_grid)
    same_tenant = tenant_grid[:, :, None] == tenant_grid[:, None, :]
    group_size = jnp.sum(same_tenant.astype(jnp.int32), axis=2)
    length_limit = CAP // group_size
    length_grid = jax.random.randint(length_key, (shard_count, SHARD_PAIRS), (length_limit + 1) // 2, length_limit + 1)
    in_group = (tenant_grid == favored) & jnp.logical_not(is_picked)
    others = jnp.sum(jnp.where(in_group, length_grid, 0), axis=1, keepdims=True)
    length_grid = jnp.where(is_picked, CAP - others, length_grid)
    return (tenant_grid.reshape(-1).astype(jnp.int32), length_grid.reshape(-1).astype(jnp.int32))


def draw_pair_tenant(key, part):
    return routing(key)[0]


def draw_pair_length(key, part):
    return routing(key)[1]


def query_key_pair(key):
    mixed_key = jax.random.fold_in(key, 29)
    first_key, second_key = jax.random.split(mixed_key, 2)
    tenant_count = PAIRS_ALL // SHARD_PAIRS
    array_shape = (tenant_count, D, HEADS * DK)
    fan_scale = 1.0 / math.sqrt(D)
    score_scale = 1.0 / math.sqrt(DK)
    first_draw = jax.random.normal(first_key, array_shape, jnp.float32) * fan_scale
    second_draw = jax.random.normal(second_key, array_shape, jnp.float32) * fan_scale
    return (jnp.clip(first_draw, -1.0, 1.0) * score_scale, jnp.clip(second_draw, -1.0, 1.0))


def draw_w_query(key, part):
    return query_key_pair(key)[0].astype(jnp.bfloat16)


def draw_w_key(key, part):
    return query_key_pair(key)[1].astype(jnp.bfloat16)


def draw_src_tokens(key, part):
    base_key = jax.random.fold_in(jax.random.fold_in(key, 41), 0)
    normal_values = jax.random.normal(base_key, (PAIRS_ALL, CAP, D), jnp.float32)
    return jnp.clip(normal_values, -6.0, 6.0).astype(jnp.bfloat16)


def block_levels(rng, shape, cuts, low, top_value):
    loudness, own = 1.0, jax.random.fold_in(rng, 6)
    for dim, shards_of in cuts:
        steps = jnp.exp(jax.random.uniform(jax.random.fold_in(own, dim), (shards_of,), jnp.float32, low / len(cuts), top_value / len(cuts)))
        loudness = loudness * jnp.repeat(steps, shape[dim] // shards_of).reshape([-1 if axis == dim else 1 for axis in range(len(shape))])
    return loudness


def bell_draw(rng, shape, width, most, cuts=(), kind=jnp.bfloat16):
    array = width * jax.random.normal(rng, shape, jnp.float32)
    if cuts:
        array = array * block_levels(rng, shape, cuts, -0.22, 0.18)
    return jnp.clip(array, -most, most).astype(kind)


def setup_inputs(seed: int = 0) -> dict:
    splits = jax.random.split(jax.random.key(seed), 10)
    return {
        "src_tokens": draw_src_tokens(jax.random.fold_in(splits[9], 71), 0),
        "pair_tenant": draw_pair_tenant(jax.random.fold_in(splits[9], 71), 0),
        "pair_length": draw_pair_length(jax.random.fold_in(splits[9], 71), 0),
        "norm_gain": jnp.clip(1.0 + 0.18 * jax.random.normal(splits[3], (N_TENANT, D), jnp.float32), 0.1, 1.9),
        "w_query": draw_w_query(jax.random.fold_in(splits[9], 71), 0),
        "w_key": draw_w_key(jax.random.fold_in(splits[9], 71), 0),
        "w_value": bell_draw(splits[6], (N_TENANT, D, HEADS * DK), D ** -0.5, 0.1875, ((0, 8), (2, 4))),
        "w_out": bell_draw(splits[7], (N_TENANT, HEADS * DK, D), (HEADS * DK) ** -0.5, 0.09375, ((0, 8), (1, 4))),
        "rel_bias": bell_draw(splits[8], (N_TENANT, BUCKETS, HEADS), 1.0, 6.0, ((0, 8), (2, 4)), jnp.float32),
    }


def bucket_grid(extent, buckets):
    offsets = np.arange(extent)[None, :] - np.arange(extent)[:, None]
    half_count = buckets // 2
    upward = np.where(offsets > 0, half_count, 0)
    distance = np.abs(offsets)
    exact_limit = half_count // 2
    ratio = np.maximum(distance, 1) / exact_limit
    spread_bucket = exact_limit + np.floor(np.log(ratio) / math.log(128.0 / exact_limit) * (half_count - exact_limit)).astype(np.int32)
    spread_bucket = np.minimum(spread_bucket, half_count - 1)
    return (upward + np.where(distance < exact_limit, distance, spread_bucket)).astype(np.int32)

def rms_normed(tenant_rows, gain_row):
    values = tenant_rows.astype(jnp.float32)
    mean_square = lax.optimization_barrier(jnp.mean(values * values, axis=-1, keepdims=True))
    return (values * lax.rsqrt(mean_square + 1e-06) * gain_row).astype(jnp.bfloat16)

def reference(src_tokens, pair_tenant, pair_length, norm_gain, w_query, w_key, w_value, w_out, rel_bias):
    shard_pairs = PAIRS_ALL // N_TENANT
    tenant_grid = pair_tenant.reshape(N_TENANT, shard_pairs).astype(jnp.int32)
    length_grid = pair_length.reshape(N_TENANT, shard_pairs).astype(jnp.int32)
    pair_order = jnp.arange(shard_pairs, dtype=jnp.int32)
    earlier = (tenant_grid[:, :, None] == tenant_grid[:, None, :]) & (pair_order[None, None, :] < pair_order[None, :, None])
    offset = lax.optimization_barrier(jnp.sum(jnp.where(earlier, length_grid[:, None, :], 0), axis=2)).astype(jnp.int32)
    source = jnp.arange(N_TENANT, dtype=jnp.int32)[:, None]
    start_row = ((tenant_grid * N_TENANT + source) * CAP + offset).astype(jnp.int32)
    position = jnp.arange(CAP, dtype=jnp.int32)
    target = start_row[:, :, None] + position[None, None, :]
    target = jnp.where(position[None, None, :] < length_grid[:, :, None], target, ROWS).reshape(-1).astype(jnp.int32)
    packed = jnp.zeros((ROWS, D), jnp.bfloat16).at[target].set(src_tokens.reshape(-1, D), mode='drop')
    pair_ids = jnp.broadcast_to(jnp.arange(PAIRS_ALL, dtype=jnp.int32)[:, None], (PAIRS_ALL, CAP)).reshape(-1)
    segment = jnp.full((ROWS,), -1, jnp.int32).at[target].set(pair_ids, mode='drop')
    bucket_index = jnp.asarray(bucket_grid(CAP, BUCKETS))
    group_width = HEADS * DK // N_TP
    tenant_count_rows = N_TENANT * CAP

    def one_tenant(inputs):
        tenant_rows, tenant_segment, gain_row, query_weight, key_weight, value_weight, out_weight, bias_table = inputs
        normed = rms_normed(tenant_rows, gain_row)
        query_rows = jnp.dot(normed, query_weight, preferred_element_type=jnp.float32).astype(jnp.bfloat16)
        key_rows = jnp.dot(normed, key_weight, preferred_element_type=jnp.float32).astype(jnp.bfloat16)
        value_rows = jnp.dot(normed, value_weight, preferred_element_type=jnp.float32).astype(jnp.bfloat16)
        query_blocks = query_rows.reshape(N_TENANT, CAP, HEADS, DK).astype(jnp.float32)
        key_blocks = key_rows.reshape(N_TENANT, CAP, HEADS, DK).astype(jnp.float32)
        value_blocks = value_rows.reshape(N_TENANT, CAP, HEADS, DK).astype(jnp.float32)
        position_bias = jnp.transpose(bias_table[bucket_index], (2, 0, 1))
        scores = jnp.einsum('bqhd,bkhd->bhqk', query_blocks, key_blocks, precision=lax.Precision.HIGHEST)
        scores = scores + position_bias[None]
        segment_blocks = tenant_segment.reshape(N_TENANT, CAP)
        allowed = (segment_blocks[:, :, None] == segment_blocks[:, None, :]) & (segment_blocks[:, None, :] >= 0)
        scores = jnp.where(allowed[:, None], scores, -1000000000.0)
        maxima = lax.optimization_barrier(jnp.max(scores, axis=-1, keepdims=True))
        weights = jnp.exp(scores - maxima)
        probabilities = (weights / lax.optimization_barrier(jnp.sum(weights, axis=-1, keepdims=True))).astype(jnp.bfloat16)
        context = jnp.einsum('bhqk,bkhd->bqhd', probabilities.astype(jnp.float32), value_blocks, precision=lax.Precision.HIGHEST)
        context = context.astype(jnp.bfloat16).reshape(tenant_count_rows, N_TP, group_width)
        partials = jnp.einsum('rgi,gid->grd', context.astype(jnp.float32), out_weight.reshape(N_TP, group_width, D).astype(jnp.float32), precision=lax.Precision.HIGHEST)
        partials = lax.optimization_barrier(partials.astype(jnp.bfloat16)).astype(jnp.float32)
        total = tenant_rows.astype(jnp.float32) + lax.optimization_barrier(jnp.sum(partials, axis=0))
        return jnp.where(tenant_segment[:, None] >= 0, total, 0.0).astype(jnp.bfloat16)
    outputs = lax.map(one_tenant, (packed.reshape(N_TENANT, tenant_count_rows, D), segment.reshape(N_TENANT, tenant_count_rows), norm_gain, w_query, w_key, w_value, w_out, rel_bias))
    return outputs.reshape(ROWS, D)
```

```python
import functools
import math

import jax
import jax.numpy as jnp
import numpy as np
from jax import lax
from jax.experimental import pallas as pl
from jax.experimental.pallas import tpu as pltpu
from jax.sharding import PartitionSpec as P


LANES = 128
SEG_ROWS = 8
BLOCK = 256
MASKED = -1000000000.0
VMEM = pl.BlockSpec(memory_space=pltpu.VMEM)
SMEM = pl.BlockSpec(memory_space=pltpu.SMEM)


def bucket_of(distance, buckets):
    half_count = buckets // 2
    exact_limit = half_count // 2
    size = abs(distance)
    if size < exact_limit:
        found = size
    else:
        found = exact_limit + int(
            np.floor(
                np.log(size / exact_limit)
                / math.log(128.0 / exact_limit)
                * (half_count - exact_limit)
            )
        )
        found = min(found, half_count - 1)
    return found + (half_count if distance > 0 else 0)


def bias_runs(extent, buckets):
    runs = []
    for distance in range(-extent + 1, extent):
        bucket = bucket_of(distance, buckets)
        if not runs or runs[-1][1] != bucket:
            runs.append((distance, bucket))
    return runs


def plan(tenants):
    half = tenants // 2
    split = half // 2
    far = [(tenants - 1 - i, tenants - 1 - i - split) for i in range(split)]
    near = [(half - 1 - i, half - 1 - i - split) for i in range(split - 1)]
    near.append((split, split))
    return far, near


def pick(core, pair):
    return pair[0] if pair[0] == pair[1] else jnp.where(core == 0, pair[0], pair[1])


def pack_kernel(rounds, cap, tenant_ref, length_ref, tokens_ref, *refs):
    out_refs, select = refs[:-1], refs[-1]
    pairs = tenant_ref.shape[0]
    columns = tokens_ref.shape[1]
    me = lax.axis_index("tenant")
    core = lax.rem(lax.axis_index("tp"), 2)
    side = LANES // cap
    lane = lax.broadcasted_iota(jnp.int32, (1, LANES), 1)
    place = lax.rem(lane, cap)
    part = lane // cap
    rows = lax.broadcasted_iota(jnp.int32, (cap, LANES), 0)
    for slot, pair in enumerate(rounds):
        bound = lax.bitwise_xor(me, jnp.int32(pick(core, pair)))
        offset = jnp.int32(0)
        seg = jnp.full((1, LANES), -1, jnp.int32)
        for group in range(pairs // side):
            first = jnp.zeros((1, LANES), jnp.int32)
            last = jnp.zeros((1, LANES), jnp.int32)
            for k in range(side):
                j = group * side + k
                live = jnp.where(tenant_ref[j] == bound, length_ref[j], 0)
                seg = jnp.where((place >= offset) & (place < offset + live), j, seg)
                first = jnp.where(part == k, offset, first)
                last = jnp.where(part == k, live, last)
                offset = offset + live
            target = jnp.where(place < last, first + place, -1)
            select[slot * cap : (slot + 1) * cap, group * LANES : (group + 1) * LANES] = (
                jnp.where(rows == target, 1.0, 0.0).astype(jnp.bfloat16)
            )
        out_refs[slot][columns // LANES * cap :, :] = jnp.broadcast_to(
            seg.astype(jnp.float32), (SEG_ROWS, LANES)
        ).astype(jnp.bfloat16)
    step = 2 * LANES
    for at in range(0, columns, step):
        packed = jnp.dot(
            select[...], tokens_ref[:, at : at + step], preferred_element_type=jnp.float32
        ).astype(jnp.bfloat16)
        for slot in range(len(rounds)):
            for c in range(step // LANES):
                block = at // LANES + c
                out_refs[slot][block * cap : (block + 1) * cap, :] = packed[
                    slot * cap : (slot + 1) * cap, c * LANES : (c + 1) * LANES
                ]


def bias_kernel(runs, table_ref, out_ref):
    heads, extent = out_ref.shape[0], out_ref.shape[1]
    distance = lax.broadcasted_iota(jnp.int32, (extent, extent), 1) - lax.broadcasted_iota(
        jnp.int32, (extent, extent), 0
    )
    for head in range(heads):
        value = jnp.full((extent, extent), table_ref[runs[0][1], head], jnp.float32)
        for start, bucket in runs[1:]:
            value = jnp.where(distance >= start, table_ref[bucket, head], value)
        out_ref[head] = value


def sublayer_kernel(slots, far, cap, slot_count, *refs):
    slot_refs = refs[:slot_count]
    gain_ref, wq_ref, wk_ref, wv_ref, wo_ref, bias_ref = refs[slot_count : slot_count + 6]
    send_ref, keep_ref, x, seg, normed, q, k, v, context = refs[slot_count + 6 :]
    half, split = slot_count, slot_count // 2
    width = x.shape[1]
    me = lax.axis_index("tenant")
    t = lax.axis_index("tp")
    core, outer = lax.rem(t, 2), t // 2
    for ref, pair in zip(slot_refs, slots):
        slot = lax.bitwise_and(lax.bitwise_xor(me, jnp.int32(pick(core, pair))), half - 1)
        at = lax.bitwise_xor(slot, (1 - core) * split)
        for c in range(width // LANES):
            x[pl.ds(pl.multiple_of(at * cap, cap), cap), c * LANES : (c + 1) * LANES] = ref[
                c * cap : (c + 1) * cap, :
            ]
        seg[at] = ref[width // LANES * cap :, :].astype(jnp.float32)
    total = half * cap
    step = min(BLOCK, total)
    inner = min(LANES, total)
    side = inner // cap
    heads = bias_ref.shape[0]
    size = q.shape[1] // heads
    lane = lax.broadcasted_iota(jnp.int32, (1, inner), 1)
    diagonal = lax.broadcasted_iota(jnp.int32, (inner, inner), 0) == lax.broadcasted_iota(
        jnp.int32, (inner, inner), 1
    )
    owner = (me // half == outer) if not far else (me // half != outer)
    scale = jnp.where(owner, 1.0, 0.0).astype(jnp.float32)
    for base in range(0, total, step):
        rows = slice(base, base + step)
        values = x[rows].astype(jnp.float32)
        mean_square = jnp.mean(values * values, axis=-1, keepdims=True)
        normed[...] = (values * lax.rsqrt(mean_square + 1e-06) * gain_ref[...]).astype(
            jnp.bfloat16
        )
        for w_ref, out in ((wq_ref, q), (wk_ref, k), (wv_ref, v)):
            out[...] = jnp.dot(
                normed[...], w_ref[...], preferred_element_type=jnp.float32
            ).astype(jnp.bfloat16)
        for block in range(step // inner):
            first = (base + block * inner) // cap
            code = jnp.full((1, inner), -1.0, jnp.float32)
            for s in range(side):
                one = seg[first + s][:1, :inner]
                one = jnp.where(one >= 0.0, one + 1024.0 * s, -1.0)
                code = jnp.where(lane // cap == s, one, code)
            down = jnp.sum(jnp.where(diagonal, code, 0.0), axis=1, keepdims=True)
            allowed = down == jnp.where(code >= 0.0, code, -2.0)
            alive = down >= 0.0
            at = slice(block * inner, (block + 1) * inner)
            for head in range(heads):
                cols = slice(head * size, (head + 1) * size)
                scores = lax.dot_general(
                    q[at, cols],
                    k[at, cols],
                    (((1,), (1,)), ((), ())),
                    preferred_element_type=jnp.float32,
                )
                scores = jnp.where(allowed, scores + bias_ref[head], MASKED)
                weights = jnp.exp(scores - jnp.max(scores, axis=-1, keepdims=True))
                share = jnp.where(alive, 1.0 / jnp.sum(weights, axis=-1, keepdims=True), 0.0)
                context[at, cols] = jnp.dot(
                    (weights * share).astype(jnp.bfloat16),
                    v[at, cols],
                    preferred_element_type=jnp.float32,
                ).astype(jnp.bfloat16)
        partial = jnp.dot(context[...], wo_ref[...], preferred_element_type=jnp.float32)
        for at in range(0, step, split * cap) if step > split * cap else (0,):
            size_out = min(step, split * cap)
            row = base + at
            piece = partial[at : at + size_out]
            if row < split * cap:
                send_ref[row : row + size_out] = piece.astype(jnp.bfloat16)
            else:
                keep_ref[row - split * cap : row - split * cap + size_out] = (
                    piece + scale * x[row : row + size_out].astype(jnp.float32)
                )


def per_device(
    tenants,
    tp,
    src_tokens,
    pair_tenant,
    pair_length,
    norm_gain,
    w_query,
    w_key,
    w_value,
    w_out,
    rel_bias,
):
    pairs, cap, width = src_tokens.shape
    half, split = tenants // 2, tenants // 4
    far, near = plan(tenants)
    rounds = far + near + [(0, 0)]
    slot_shape = jax.ShapeDtypeStruct((width // LANES * cap + SEG_ROWS, LANES), jnp.bfloat16)
    packed = pl.pallas_call(
        functools.partial(pack_kernel, rounds, cap),
        out_shape=[slot_shape] * len(rounds),
        in_specs=[SMEM, SMEM, VMEM],
        out_specs=[VMEM] * len(rounds),
        scratch_shapes=[pltpu.VMEM((len(rounds) * cap, pairs * cap), jnp.bfloat16)],
        name="pack",
    )(pair_tenant, pair_length, src_tokens.reshape(pairs * cap, width))

    def shift(value, pair):
        moves = []
        for u in range(tenants):
            for t in range(tp):
                moves.append((u * tp + t, (u ^ pair[t % 2]) * tp + t))
        return lax.ppermute(value, ("tenant", "tp"), moves)

    def swap(value):
        return lax.ppermute(value, "tp", [(t, t ^ 1) for t in range(tp)])

    arrived = [shift(value, pair) for value, pair in zip(packed, rounds[:-1])]

    heads = rel_bias.shape[2]
    extent = min(LANES, half * cap)
    bias = pl.pallas_call(
        functools.partial(bias_kernel, bias_runs(extent, rel_bias.shape[1])),
        out_shape=jax.ShapeDtypeStruct((heads, extent, extent), jnp.float32),
        in_specs=[SMEM],
        out_specs=VMEM,
        name="bias",
    )(rel_bias[0])

    def sublayer(rounds_here, values, is_far):
        slots, arrays = [], []
        for pair, value in zip(rounds_here, values):
            slots.append(pair)
            arrays.append(value)
            if pair[0] != pair[1]:
                slots.append(pair[::-1])
                arrays.append(swap(value))
        total = half * cap
        step = min(BLOCK, total)
        own = w_query.shape[2]
        return pl.pallas_call(
            functools.partial(sublayer_kernel, slots, is_far, cap, half),
            out_shape=[
                jax.ShapeDtypeStruct((split * cap, width), jnp.bfloat16),
                jax.ShapeDtypeStruct((split * cap, width), jnp.float32),
            ],
            in_specs=[VMEM] * (half + 6),
            out_specs=[VMEM, VMEM],
            scratch_shapes=[
                pltpu.VMEM((total, width), jnp.bfloat16),
                pltpu.VMEM((half, SEG_ROWS, LANES), jnp.float32),
                pltpu.VMEM((step, width), jnp.bfloat16),
                pltpu.VMEM((step, own), jnp.bfloat16),
                pltpu.VMEM((step, own), jnp.bfloat16),
                pltpu.VMEM((step, own), jnp.bfloat16),
                pltpu.VMEM((step, own), jnp.bfloat16),
            ],
            name="far" if is_far else "near",
        )(*arrays, norm_gain, w_query[0], w_key[0], w_value[0], w_out[0], bias)

    def cross(value, is_far):
        moves = []
        for u in range(tenants):
            for t in range(tp):
                owner = (u // half == t // 2) != is_far
                if not owner:
                    moves.append((u * tp + t, u * tp + (t ^ 2)))
        return lax.ppermute(value, ("tenant", "tp"), moves)

    def reduced(rounds_here, values, is_far):
        send, keep = sublayer(rounds_here, values, is_far)
        pair_sum = keep + swap(send).astype(jnp.float32)
        return pair_sum, cross(pair_sum.astype(jnp.bfloat16), is_far)

    near_sum, near_other = reduced(near + [(0, 0)], arrived[len(far) :] + [packed[-1]], False)
    far_sum, far_other = reduced(far, arrived[: len(far)], True)
    owner = lax.axis_index("tenant") // half == lax.axis_index("tp") // 2
    return jnp.where(
        owner,
        near_sum + near_other.astype(jnp.float32),
        far_sum + far_other.astype(jnp.float32),
    ).astype(jnp.bfloat16)


def solution(mesh):
    in_specs = (
        P("tenant", None, None),
        P("tenant"),
        P("tenant"),
        P("tenant", None),
        P("tenant", None, "tp"),
        P("tenant", None, "tp"),
        P("tenant", None, "tp"),
        P("tenant", "tp", None),
        P("tenant", None, "tp"),
    )
    out_specs = P(("tenant", "tp"), None)
    return jax.shard_map(
        functools.partial(per_device, mesh.shape["tenant"], mesh.shape["tp"]),
        mesh=mesh,
        in_specs=in_specs,
        out_specs=out_specs,
        check_vma=False,
    )
```

```python
import functools
import math

import jax
import jax.numpy as jnp
import numpy as np
from jax import lax
from jax.experimental import pallas as pl
from jax.experimental.pallas import tpu as pltpu
from jax.sharding import PartitionSpec as P


LANES = 128
SEG_ROWS = 8
BLOCK = 256
MASKED = -1000000000.0
VMEM = pl.BlockSpec(memory_space=pltpu.VMEM)
SMEM = pl.BlockSpec(memory_space=pltpu.SMEM)
HBM = pl.BlockSpec(memory_space=pltpu.HBM)
MIB = 2**20


def in_vmem(value):
    return pltpu.with_memory_space_constraint(value, pltpu.VMEM)


def in_hbm(value):
    return pltpu.with_memory_space_constraint(value, pltpu.HBM)


def bucket_of(distance, buckets):
    half_count = buckets // 2
    exact_limit = half_count // 2
    size = abs(distance)
    if size < exact_limit:
        found = size
    else:
        found = exact_limit + int(
            np.floor(
                np.log(size / exact_limit)
                / math.log(128.0 / exact_limit)
                * (half_count - exact_limit)
            )
        )
        found = min(found, half_count - 1)
    return found + (half_count if distance > 0 else 0)


def bias_runs(extent, buckets):
    runs = []
    for distance in range(-extent + 1, extent):
        bucket = bucket_of(distance, buckets)
        if not runs or runs[-1][1] != bucket:
            runs.append((distance, bucket))
    return runs


def plan(tenants):
    half = tenants // 2
    split = half // 2
    far = [(tenants - 1 - i, tenants - 1 - i - split) for i in range(split)]
    near = [(half - 1 - i, half - 1 - i - split) for i in range(split - 1)]
    near.append((split, split))
    return far, near


def pick(core, pair):
    return pair[0] if pair[0] == pair[1] else jnp.where(core == 0, pair[0], pair[1])


def pack_kernel(rounds, cap, tenant_hbm, length_hbm, tokens_hbm, *refs):
    out_refs = refs[:-5]
    select, tokens_ref, tenant_ref, length_ref, semaphore = refs[-5:]
    pairs = tenant_ref.shape[0]
    columns = tokens_ref.shape[1]
    tables = [
        pltpu.make_async_copy(tenant_hbm, tenant_ref, semaphore.at[0]),
        pltpu.make_async_copy(length_hbm, length_ref, semaphore.at[1]),
    ]
    for copy in tables:
        copy.start()
    step = 2 * LANES
    fetches = []
    for i, at in enumerate(range(0, columns, step)):
        where = slice(at, at + step)
        fetches.append(
            pltpu.make_async_copy(
                tokens_hbm.at[:, where], tokens_ref.at[:, where], semaphore.at[2 + i]
            )
        )
        fetches[-1].start()
    for copy in tables:
        copy.wait()
    me = lax.axis_index("tenant")
    core = lax.rem(lax.axis_index("tp"), 2)
    side = LANES // cap
    lane = lax.broadcasted_iota(jnp.int32, (1, LANES), 1)
    place = lax.rem(lane, cap)
    part = lane // cap
    rows = lax.broadcasted_iota(jnp.int32, (cap, LANES), 0)
    for slot, pair in enumerate(rounds):
        bound = lax.bitwise_xor(me, jnp.int32(pick(core, pair)))
        offset = jnp.int32(0)
        seg = jnp.full((1, LANES), -1, jnp.int32)
        for group in range(pairs // side):
            first = jnp.zeros((1, LANES), jnp.int32)
            last = jnp.zeros((1, LANES), jnp.int32)
            for k in range(side):
                j = group * side + k
                live = jnp.where(tenant_ref[j] == bound, length_ref[j], 0)
                seg = jnp.where((place >= offset) & (place < offset + live), j, seg)
                first = jnp.where(part == k, offset, first)
                last = jnp.where(part == k, live, last)
                offset = offset + live
            target = jnp.where(place < last, first + place, -1)
            select[slot * cap : (slot + 1) * cap, group * LANES : (group + 1) * LANES] = (
                jnp.where(rows == target, 1.0, 0.0).astype(jnp.bfloat16)
            )
        out_refs[slot][columns // LANES * cap :, :] = jnp.broadcast_to(
            seg.astype(jnp.float32), (SEG_ROWS, LANES)
        ).astype(jnp.bfloat16)
    for fetch, at in zip(fetches, range(0, columns, step)):
        fetch.wait()
        packed = jnp.dot(
            select[...], tokens_ref[:, at : at + step], preferred_element_type=jnp.float32
        ).astype(jnp.bfloat16)
        for slot in range(len(rounds)):
            for c in range(step // LANES):
                block = at // LANES + c
                out_refs[slot][block * cap : (block + 1) * cap, :] = packed[
                    slot * cap : (slot + 1) * cap, c * LANES : (c + 1) * LANES
                ]


def prepare_kernel(runs, table_ref, *refs):
    count = (len(refs) - 2) // 2
    sources, bias_ref, targets, semaphore = refs[:count], refs[count], refs[count + 1 : -1], refs[-1]
    copies = []
    for i, (source, target) in enumerate(zip(sources, targets)):
        copies.append(pltpu.make_async_copy(source, target, semaphore.at[i]))
        copies[-1].start()
    heads, extent = bias_ref.shape[0], bias_ref.shape[1]
    distance = lax.broadcasted_iota(jnp.int32, (extent, extent), 1) - lax.broadcasted_iota(
        jnp.int32, (extent, extent), 0
    )
    for head in range(heads):
        value = jnp.full((extent, extent), table_ref[head, runs[0][1]], jnp.float32)
        for start, bucket in runs[1:]:
            value = jnp.where(distance >= start, table_ref[head, bucket], value)
        bias_ref[head] = value
    for copy in copies:
        copy.wait()


def sublayer_kernel(slots, far, cap, slot_count, *refs):
    slot_refs = refs[:slot_count]
    gain_ref, wq_ref, wk_ref, wv_ref, wo_ref, bias_ref = refs[slot_count : slot_count + 6]
    send_ref, keep_ref, x, seg, normed, q, k, v, context, score, top, weight = refs[
        slot_count + 6 :
    ]
    half, split = slot_count, slot_count // 2
    width = x.shape[1]
    me = lax.axis_index("tenant")
    t = lax.axis_index("tp")
    core, outer = lax.rem(t, 2), t // 2
    for ref, pair in zip(slot_refs, slots):
        slot = lax.bitwise_and(lax.bitwise_xor(me, jnp.int32(pick(core, pair))), half - 1)
        at = lax.bitwise_xor(slot, (1 - core) * split)
        for c in range(width // LANES):
            x[pl.ds(pl.multiple_of(at * cap, cap), cap), c * LANES : (c + 1) * LANES] = ref[
                c * cap : (c + 1) * cap, :
            ]
        seg[at] = ref[width // LANES * cap :, :].astype(jnp.float32)
    total = half * cap
    step = min(BLOCK, total)
    inner = min(LANES, total)
    side = inner // cap
    heads = bias_ref.shape[0]
    size = q.shape[1] // heads
    lane = lax.broadcasted_iota(jnp.int32, (1, inner), 1)
    diagonal = lax.broadcasted_iota(jnp.int32, (inner, inner), 0) == lax.broadcasted_iota(
        jnp.int32, (inner, inner), 1
    )
    owner = (me // half == outer) if not far else (me // half != outer)
    ones = jnp.ones((inner, size), jnp.bfloat16)
    scale = jnp.where(owner, 1.0, 0.0).astype(jnp.float32)
    for base in range(0, total, step):
        rows = slice(base, base + step)
        values = x[rows].astype(jnp.float32)
        mean_square = jnp.mean(values * values, axis=-1, keepdims=True)
        normed[...] = (values * lax.rsqrt(mean_square + 1e-06) * gain_ref[...]).astype(
            jnp.bfloat16
        )
        for w_ref, out in ((wq_ref, q), (wk_ref, k), (wv_ref, v)):
            out[...] = jnp.dot(
                normed[...], w_ref[...], preferred_element_type=jnp.float32
            ).astype(jnp.bfloat16)
        blocks = step // inner
        for block in range(blocks):
            first = (base + block * inner) // cap
            code = jnp.full((1, inner), -1.0, jnp.float32)
            for s in range(side):
                one = seg[first + s][:1, :inner]
                one = jnp.where(one >= 0.0, one + 1024.0 * s, -1.0)
                code = jnp.where(lane // cap == s, one, code)
            down = jnp.sum(jnp.where(diagonal, code, 0.0), axis=1, keepdims=True)
            allowed = down == jnp.where(code >= 0.0, code, -2.0)
            alive = jnp.broadcast_to(down >= 0.0, (inner, inner))
            at = slice(block * inner, (block + 1) * inner)
            for head in range(heads):
                cols = slice(head * size, (head + 1) * size)
                scores = lax.dot_general(
                    q[at, cols],
                    k[at, cols],
                    (((1,), (1,)), ((), ())),
                    preferred_element_type=jnp.float32,
                )
                scores = jnp.where(allowed, scores + bias_ref[head], MASKED)
                score[head] = scores
                top[head] = jnp.broadcast_to(
                    jnp.max(scores, axis=-1, keepdims=True), (inner, inner)
                )
            for head in range(heads):
                weight[head] = jnp.exp(score[head] - top[head]).astype(jnp.bfloat16)
            for head in range(heads):
                cols = slice(head * size, (head + 1) * size)
                both = jnp.dot(
                    weight[head],
                    jnp.concatenate([v[at, cols], ones], axis=1),
                    preferred_element_type=jnp.float32,
                )
                context[at, cols] = jnp.where(
                    alive, both[:, :size] * (1.0 / both[:, size:]), 0.0
                ).astype(jnp.bfloat16)
        partial = jnp.dot(context[...], wo_ref[...], preferred_element_type=jnp.float32)
        for at in range(0, step, split * cap) if step > split * cap else (0,):
            size_out = min(step, split * cap)
            row = base + at
            piece = partial[at : at + size_out]
            if row < split * cap:
                send_ref[row : row + size_out] = piece.astype(jnp.bfloat16)
            else:
                keep_ref[row - split * cap : row - split * cap + size_out] = (
                    piece + scale * x[row : row + size_out].astype(jnp.float32)
                )


def per_device(
    tenants,
    tp,
    src_tokens,
    pair_tenant,
    pair_length,
    norm_gain,
    w_query,
    w_key,
    w_value,
    w_out,
    rel_bias,
):
    pairs, cap, width = src_tokens.shape
    half, split = tenants // 2, tenants // 4
    far, near = plan(tenants)
    rounds = far + near + [(0, 0)]
    slot_shape = pltpu.VMEM((width // LANES * cap + SEG_ROWS, LANES), jnp.bfloat16)
    packed = pl.pallas_call(
        functools.partial(pack_kernel, rounds, cap),
        out_shape=[slot_shape] * len(rounds),
        in_specs=[HBM, HBM, HBM],
        out_specs=[VMEM] * len(rounds),
        scratch_shapes=[
            pltpu.VMEM((len(rounds) * cap, pairs * cap), jnp.bfloat16),
            pltpu.VMEM((pairs * cap, width), jnp.bfloat16),
            pltpu.SMEM((pairs,), jnp.int32),
            pltpu.SMEM((pairs,), jnp.int32),
            pltpu.SemaphoreType.DMA((2 + width // (2 * LANES),)),
        ],
        compiler_params=pltpu.CompilerParams(
            vmem_limit_bytes=2 * MIB + 2 * pairs * cap * (width + (len(rounds) + 1) * cap)
        ),
        name="pack",
    )(*map(in_hbm, (pair_tenant, pair_length, src_tokens.reshape(pairs * cap, width))))

    def shift(value, pair):
        moves = []
        for u in range(tenants):
            for t in range(tp):
                moves.append((u * tp + t, (u ^ pair[t % 2]) * tp + t))
        return lax.ppermute(value, ("tenant", "tp"), moves)

    def swap(value):
        return lax.ppermute(value, "tp", [(t, t ^ 1) for t in range(tp)])

    arrived = []
    for value, pair in zip(packed, rounds[:-1]):
        arrived.append(shift(value, pair))

    heads = rel_bias.shape[2]
    extent = min(LANES, half * cap)
    raw = [w[0] for w in (w_query, w_key, w_value, w_out)]
    bias, *weights = pl.pallas_call(
        functools.partial(prepare_kernel, bias_runs(extent, rel_bias.shape[1])),
        out_shape=[pltpu.VMEM((heads, extent, extent), jnp.float32)]
        + [pltpu.VMEM(w.shape, w.dtype) for w in raw],
        in_specs=[SMEM] + [HBM] * len(raw),
        out_specs=[VMEM] * (1 + len(raw)),
        scratch_shapes=[pltpu.SemaphoreType.DMA((len(raw),))],
        compiler_params=pltpu.CompilerParams(vmem_limit_bytes=4 * MIB),
        name="prepare",
    )(rel_bias[0].T, *map(in_hbm, raw))

    def sublayer(rounds_here, values, is_far):
        slots, arrays = [], []
        for pair, value in zip(rounds_here, values):
            slots.append(pair)
            arrays.append(value)
            if pair[0] != pair[1]:
                slots.append(pair[::-1])
                arrays.append(swap(value))
        total = half * cap
        step = min(BLOCK, total)
        own = w_query.shape[2]
        vmem = 8 * MIB + 4 * total * width
        return pl.pallas_call(
            functools.partial(sublayer_kernel, slots, is_far, cap, half),
            out_shape=[
                pltpu.VMEM((split * cap, width), jnp.bfloat16),
                pltpu.VMEM((split * cap, width), jnp.float32),
            ],
            in_specs=[VMEM] * (half + 6),
            out_specs=[VMEM, VMEM],
            scratch_shapes=[
                pltpu.VMEM((total, width), jnp.bfloat16),
                pltpu.VMEM((half, SEG_ROWS, LANES), jnp.float32),
                pltpu.VMEM((step, width), jnp.bfloat16),
                pltpu.VMEM((step, own), jnp.bfloat16),
                pltpu.VMEM((step, own), jnp.bfloat16),
                pltpu.VMEM((step, own), jnp.bfloat16),
                pltpu.VMEM((step, own), jnp.bfloat16),
                pltpu.VMEM((heads, extent, extent), jnp.float32),
                pltpu.VMEM((heads, extent, extent), jnp.float32),
                pltpu.VMEM((heads, extent, extent), jnp.bfloat16),
            ],
            compiler_params=pltpu.CompilerParams(vmem_limit_bytes=vmem),
            name="far" if is_far else "near",
        )(*[in_vmem(value) for value in arrays], norm_gain, *map(in_vmem, weights), in_vmem(bias))

    def cross(value, is_far):
        moves = []
        for u in range(tenants):
            for t in range(tp):
                owner = (u // half == t // 2) != is_far
                if not owner:
                    moves.append((u * tp + t, u * tp + (t ^ 2)))
        return lax.ppermute(value, ("tenant", "tp"), moves)

    def reduced(rounds_here, values, is_far):
        send, keep = sublayer(rounds_here, values, is_far)
        other = swap(send)
        pair_sum = keep + other.astype(jnp.float32)
        return pair_sum, cross(pair_sum.astype(jnp.bfloat16), is_far)

    near_sum, near_other = reduced(near + [(0, 0)], arrived[len(far) :] + [packed[-1]], False)
    far_sum, far_other = reduced(far, arrived[: len(far)], True)
    owner = lax.axis_index("tenant") // half == lax.axis_index("tp") // 2
    return jnp.where(
        owner,
        near_sum + near_other.astype(jnp.float32),
        far_sum + far_other.astype(jnp.float32),
    ).astype(jnp.bfloat16)


def solution(mesh):
    in_specs = (
        P("tenant", None, None),
        P("tenant"),
        P("tenant"),
        P("tenant", None),
        P("tenant", None, "tp"),
        P("tenant", None, "tp"),
        P("tenant", None, "tp"),
        P("tenant", "tp", None),
        P("tenant", None, "tp"),
    )
    out_specs = P(("tenant", "tp"), None)
    tenants = mesh.shape["tenant"]

    def body(*args):
        return per_device(tenants, mesh.shape["tp"], *args)

    return jax.shard_map(
        body, mesh=mesh, in_specs=in_specs, out_specs=out_specs, check_vma=False
    )
```

```python
import functools
import math

import jax
import jax.numpy as jnp
import numpy as np
from jax import lax
from jax.experimental import pallas as pl
from jax.experimental.pallas import tpu as pltpu
from jax.sharding import PartitionSpec as P


LANES = 128
SEG_ROWS = 8
BLOCK = 256
MASKED = -1000000000.0
VMEM = pl.BlockSpec(memory_space=pltpu.VMEM)
SMEM = pl.BlockSpec(memory_space=pltpu.SMEM)
HBM = pl.BlockSpec(memory_space=pltpu.HBM)
MIB = 2**20


def in_vmem(value):
    return pltpu.with_memory_space_constraint(value, pltpu.VMEM)


def in_hbm(value):
    return pltpu.with_memory_space_constraint(value, pltpu.HBM)


def bucket_of(distance, buckets):
    half_count = buckets // 2
    exact_limit = half_count // 2
    size = abs(distance)
    if size < exact_limit:
        found = size
    else:
        found = exact_limit + int(
            np.floor(
                np.log(size / exact_limit)
                / math.log(128.0 / exact_limit)
                * (half_count - exact_limit)
            )
        )
        found = min(found, half_count - 1)
    return found + (half_count if distance > 0 else 0)


def bias_runs(extent, buckets):
    runs = []
    for distance in range(-extent + 1, extent):
        bucket = bucket_of(distance, buckets)
        if not runs or runs[-1][1] != bucket:
            runs.append((distance, bucket))
    return runs


def plan(tenants):
    half = tenants // 2
    split = half // 2
    far = [(tenants - 1 - i, tenants - 1 - i - split) for i in range(split)]
    near = [(half - 1 - i, half - 1 - i - split) for i in range(split - 1)]
    near.append((split, split))
    return far, near


def pick(core, pair):
    return pair[0] if pair[0] == pair[1] else jnp.where(core == 0, pair[0], pair[1])


def pack_kernel(rounds, cap, runs, tenant_hbm, length_hbm, table_hbm, tokens_hbm, *refs):
    out_refs, strip_ref = refs[:-7], refs[-7]
    select, tokens_ref, tenant_ref, length_ref, table_ref, semaphore = refs[-6:]
    pairs = tenant_ref.shape[0]
    columns = tokens_ref.shape[1]
    tables = [
        pltpu.make_async_copy(tenant_hbm, tenant_ref, semaphore.at[0]),
        pltpu.make_async_copy(length_hbm, length_ref, semaphore.at[1]),
        pltpu.make_async_copy(table_hbm, table_ref, semaphore.at[2]),
    ]
    for copy in tables:
        copy.start()
    step = columns // 2
    fetches = []
    for i, at in enumerate(range(0, columns, step)):
        where = slice(at, at + step)
        fetches.append(
            pltpu.make_async_copy(
                tokens_hbm.at[:, where], tokens_ref.at[:, where], semaphore.at[3 + i]
            )
        )
        fetches[-1].start()
    for copy in tables:
        copy.wait()
    me = lax.axis_index("tenant")
    core = lax.rem(lax.axis_index("tp"), 2)
    side = LANES // cap
    lane = lax.broadcasted_iota(jnp.int32, (1, LANES), 1)
    place = lax.rem(lane, cap)
    part = lane // cap
    rows = lax.broadcasted_iota(jnp.int32, (cap, LANES), 0)
    for slot, pair in enumerate(rounds):
        bound = lax.bitwise_xor(me, jnp.int32(pick(core, pair)))
        offset = jnp.int32(0)
        seg = jnp.full((1, LANES), -1, jnp.int32)
        for group in range(pairs // side):
            first = jnp.zeros((1, LANES), jnp.int32)
            last = jnp.zeros((1, LANES), jnp.int32)
            for k in range(side):
                j = group * side + k
                live = jnp.where(tenant_ref[j] == bound, length_ref[j], 0)
                seg = jnp.where((place >= offset) & (place < offset + live), j, seg)
                first = jnp.where(part == k, offset, first)
                last = jnp.where(part == k, live, last)
                offset = offset + live
            target = jnp.where(place < last, first + place, -1)
            select[slot * cap : (slot + 1) * cap, group * LANES : (group + 1) * LANES] = (
                jnp.where(rows == target, 1.0, 0.0).astype(jnp.bfloat16)
            )
        out_refs[slot][columns // LANES * cap :, :] = jnp.broadcast_to(
            seg.astype(jnp.float32), (SEG_ROWS, LANES)
        ).astype(jnp.bfloat16)
    heads, band, double = strip_ref.shape
    distance = (
        lax.broadcasted_iota(jnp.int32, (band, double), 1)
        - lax.broadcasted_iota(jnp.int32, (band, double), 0)
        - double // 2
    )
    for head in range(heads):
        strip = jnp.full(distance.shape, table_ref[head, runs[0][1]], jnp.float32)
        for start, bucket in runs[1:]:
            strip = jnp.where(distance >= start, table_ref[head, bucket], strip)
        strip_ref[head] = strip
    for fetch, at in zip(fetches, range(0, columns, step)):
        fetch.wait()
        packed = jnp.dot(
            select[...], tokens_ref[:, at : at + step], preferred_element_type=jnp.float32
        ).astype(jnp.bfloat16)
        for slot in range(len(rounds)):
            for c in range(step // LANES):
                block = at // LANES + c
                out_refs[slot][block * cap : (block + 1) * cap, :] = packed[
                    slot * cap : (slot + 1) * cap, c * LANES : (c + 1) * LANES
                ]


def bias_kernel(strip_ref, bias_ref):
    heads, band, double = strip_ref.shape
    extent = double // 2
    for head in range(heads):
        strip = strip_ref[head]
        for row in range(0, extent, band):
            turned = pltpu.roll(strip, (row - extent) % double, 1)
            bias_ref[head, row : row + band] = turned[:, :extent]


def sublayer_kernel(slots, far, half, cap, *refs):
    count, split = len(slots), half // 2
    slot_refs = refs[:count]
    gain_ref, wq_ref, wk_ref, wv_ref, wo_ref, bias_ref, send_ref, keep_ref = refs[
        count : count + 8
    ]
    x, seg, normed, q, k, v, context, score, top, weight = refs[count + 8 :]
    width = x.shape[1]
    part = count // 2
    me = lax.axis_index("tenant")
    t = lax.axis_index("tp")
    core, outer = lax.rem(t, 2), t // 2
    for ref, pair in zip(slot_refs, slots):
        mine = lax.rem(lax.bitwise_xor(me, jnp.int32(pick(core, pair))) // split, 2) == core
        at = jnp.where(mine, part, 0) + (pair[0] % part)
        for c in range(width // LANES):
            x[pl.ds(pl.multiple_of(at * cap, cap), cap), c * LANES : (c + 1) * LANES] = ref[
                c * cap : (c + 1) * cap, :
            ]
        seg[at] = ref[width // LANES * cap :, :].astype(jnp.float32)
    total = count * cap
    step = min(BLOCK, total)
    inner = min(LANES, total)
    side = inner // cap
    heads = bias_ref.shape[0]
    size = q.shape[1] // heads
    lane = lax.broadcasted_iota(jnp.int32, (1, inner), 1)
    diagonal = lax.broadcasted_iota(jnp.int32, (inner, inner), 0) == lax.broadcasted_iota(
        jnp.int32, (inner, inner), 1
    )
    owner = (me // half == outer) if not far else (me // half != outer)
    ones = jnp.ones((inner, size), jnp.bfloat16)
    scale = jnp.where(owner, 1.0, 0.0).astype(jnp.float32)
    for base in range(0, total, step):
        rows = slice(base, base + step)
        values = x[rows].astype(jnp.float32)
        mean_square = jnp.mean(values * values, axis=-1, keepdims=True)
        normed[...] = (values * lax.rsqrt(mean_square + 1e-06) * gain_ref[...]).astype(
            jnp.bfloat16
        )
        for w_ref, out in ((wq_ref, q), (wk_ref, k), (wv_ref, v)):
            out[...] = jnp.dot(
                normed[...], w_ref[...], preferred_element_type=jnp.float32
            ).astype(jnp.bfloat16)
        blocks = step // inner
        for block in range(blocks):
            first = (base + block * inner) // cap
            code = jnp.full((1, inner), -1.0, jnp.float32)
            for s in range(side):
                one = seg[first + s][:1, :inner]
                one = jnp.where(one >= 0.0, one + 1024.0 * s, -1.0)
                code = jnp.where(lane // cap == s, one, code)
            down = jnp.sum(jnp.where(diagonal, code, 0.0), axis=1, keepdims=True)
            allowed = down == jnp.where(code >= 0.0, code, -2.0)
            alive = jnp.broadcast_to(down >= 0.0, (inner, inner))
            at = slice(block * inner, (block + 1) * inner)
            for head in range(heads):
                cols = slice(head * size, (head + 1) * size)
                scores = lax.dot_general(
                    q[at, cols],
                    k[at, cols],
                    (((1,), (1,)), ((), ())),
                    preferred_element_type=jnp.float32,
                )
                scores = jnp.where(allowed, scores + bias_ref[head], MASKED)
                score[head] = scores
                top[head] = jnp.broadcast_to(
                    jnp.max(scores, axis=-1, keepdims=True), (inner, inner)
                )
            for head in range(heads):
                weight[head] = jnp.exp(score[head] - top[head]).astype(jnp.bfloat16)
            for head in range(heads):
                cols = slice(head * size, (head + 1) * size)
                both = jnp.dot(
                    weight[head],
                    jnp.concatenate([v[at, cols], ones], axis=1),
                    preferred_element_type=jnp.float32,
                )
                context[at, cols] = jnp.where(
                    alive, both[:, :size] * (1.0 / both[:, size:]), 0.0
                ).astype(jnp.bfloat16)
        partial = jnp.dot(context[...], wo_ref[...], preferred_element_type=jnp.float32)
        size_out = min(step, part * cap)
        for at in range(0, step, size_out):
            row = base + at
            piece = partial[at : at + size_out]
            if row < part * cap:
                send_ref[row : row + size_out] = piece.astype(jnp.bfloat16)
            else:
                keep_ref[row - part * cap : row - part * cap + size_out] = (
                    piece + scale * x[row : row + size_out].astype(jnp.float32)
                )


def join_kernel(relative, near_keep, near_got, far_keep, far_got, own_ref, send_ref):
    cap = far_keep.shape[0]
    rows = slice(relative * cap, (relative + 1) * cap)
    half = lax.axis_size("tenant") // 2
    owner = lax.axis_index("tenant") // half == lax.axis_index("tp") // 2
    near = near_keep[rows] + near_got[rows].astype(jnp.float32)
    far = far_keep[...] + far_got[...].astype(jnp.float32)
    own_ref[...] = jnp.where(owner, near, far)
    send_ref[...] = jnp.where(owner, far, near).astype(jnp.bfloat16)


def finish_kernel(cap, *refs):
    pieces = len(refs) // 2
    own_refs, other_refs, out_ref = refs[:pieces], refs[pieces:-1], refs[-1]
    me = lax.axis_index("tenant")
    for i in range(pieces):
        at = lax.bitwise_xor(lax.rem(me, pieces), pieces - 1 - i)
        out_ref[pl.ds(pl.multiple_of(at * cap, cap), cap), :] = (
            own_refs[i][...] + other_refs[i][...].astype(jnp.float32)
        ).astype(jnp.bfloat16)


def per_device(
    tenants,
    tp,
    src_tokens,
    pair_tenant,
    pair_length,
    norm_gain,
    w_query,
    w_key,
    w_value,
    w_out,
    rel_bias,
):
    pairs, cap, width = src_tokens.shape
    half, split = tenants // 2, tenants // 4
    far, near = plan(tenants)
    rounds = near + far + [(0, 0)]
    slot_shape = pltpu.VMEM((width // LANES * cap + SEG_ROWS, LANES), jnp.bfloat16)
    buckets, heads = rel_bias.shape[1:]
    extent = min(LANES, half * cap)
    *packed, strips = pl.pallas_call(
        functools.partial(pack_kernel, rounds, cap, bias_runs(extent, buckets)),
        out_shape=[slot_shape] * len(rounds)
        + [pltpu.VMEM((heads, 8, 2 * extent), jnp.float32)],
        in_specs=[HBM] * 4,
        out_specs=[VMEM] * (len(rounds) + 1),
        scratch_shapes=[
            pltpu.VMEM((len(rounds) * cap, pairs * cap), jnp.bfloat16),
            pltpu.VMEM((pairs * cap, width), jnp.bfloat16),
            pltpu.SMEM((pairs,), jnp.int32),
            pltpu.SMEM((pairs,), jnp.int32),
            pltpu.SMEM((heads, buckets), jnp.float32),
            pltpu.SemaphoreType.DMA((5,)),
        ],
        compiler_params=pltpu.CompilerParams(
            vmem_limit_bytes=2 * MIB + 2 * pairs * cap * (width + (len(rounds) + 1) * cap)
        ),
        name="pack",
    )(
        *map(
            in_hbm,
            (
                pair_tenant,
                pair_length,
                rel_bias[0].T,
                src_tokens.reshape(pairs * cap, width),
            ),
        )
    )

    def shift(value, pair):
        moves = []
        for u in range(tenants):
            for t in range(tp):
                moves.append((u * tp + t, (u ^ pair[t % 2]) * tp + t))
        return lax.ppermute(value, ("tenant", "tp"), moves)

    def swap(value):
        return lax.ppermute(value, "tp", [(t, t ^ 1) for t in range(tp)])

    arrived = []
    for value, pair in zip(packed, rounds[:-1]):
        arrived.append(shift(value, pair))

    weights = [w[0] for w in (w_query, w_key, w_value, w_out)]
    bias = pl.pallas_call(
        bias_kernel,
        out_shape=pltpu.VMEM((heads, extent, extent), jnp.float32),
        in_specs=[VMEM],
        out_specs=VMEM,
        compiler_params=pltpu.CompilerParams(vmem_limit_bytes=4 * MIB),
        cost_estimate=pl.CostEstimate(
            flops=10**10, bytes_accessed=0, transcendentals=0
        ),
        name="prepare",
    )(in_vmem(strips))

    def sublayer(rounds_here, values, is_far):
        slots, arrays = [], []
        for pair, value in zip(rounds_here, values):
            slots.append(pair)
            arrays.append(value)
            if pair[0] != pair[1]:
                slots.append(pair[::-1])
                arrays.append(swap(value))
        count = len(slots)
        total = count * cap
        step = min(BLOCK, total)
        inner = min(LANES, total)
        own = w_query.shape[2]
        send, keep = pl.pallas_call(
            functools.partial(sublayer_kernel, slots, is_far, half, cap),
            out_shape=[
                pltpu.VMEM((total // 2, width), jnp.bfloat16),
                pltpu.VMEM((total // 2, width), jnp.float32),
            ],
            in_specs=[VMEM] * (count + 6),
            out_specs=[VMEM] * 2,
            scratch_shapes=[
                pltpu.VMEM((total, width), jnp.bfloat16),
                pltpu.VMEM((count, SEG_ROWS, LANES), jnp.float32),
                pltpu.VMEM((step, width), jnp.bfloat16),
                pltpu.VMEM((step, own), jnp.bfloat16),
                pltpu.VMEM((step, own), jnp.bfloat16),
                pltpu.VMEM((step, own), jnp.bfloat16),
                pltpu.VMEM((step, own), jnp.bfloat16),
                pltpu.VMEM((heads, inner, inner), jnp.float32),
                pltpu.VMEM((heads, inner, inner), jnp.float32),
                pltpu.VMEM((heads, inner, inner), jnp.bfloat16),
            ],
            compiler_params=pltpu.CompilerParams(
                vmem_limit_bytes=6 * MIB + 4 * total * width
            ),
        )(
            *map(in_vmem, arrays),
            norm_gain,
            *map(in_vmem, weights),
            in_vmem(bias),
        )
        return keep, swap(send)

    near_sums = sublayer(near + [(0, 0)], arrived[: len(near)] + [packed[-1]], False)
    own, others = [], []
    for i, pair in enumerate(far):
        far_sums = sublayer([pair], [arrived[len(near) + i]], True)
        kept, send = pl.pallas_call(
            functools.partial(join_kernel, split - 1 - i),
            out_shape=[
                pltpu.VMEM((cap, width), jnp.float32),
                pltpu.VMEM((cap, width), jnp.bfloat16),
            ],
            in_specs=[VMEM] * 4,
            out_specs=[VMEM] * 2,
            compiler_params=pltpu.CompilerParams(vmem_limit_bytes=MIB),
        )(*map(in_vmem, (*near_sums, *far_sums)))
        others.append(lax.ppermute(send, "tp", [(t, t ^ 2) for t in range(tp)]))
        own.append(kept)
    return pl.pallas_call(
        functools.partial(finish_kernel, cap),
        out_shape=jax.ShapeDtypeStruct((split * cap, width), jnp.bfloat16),
        in_specs=[VMEM] * (2 * split),
        out_specs=VMEM,
        compiler_params=pltpu.CompilerParams(vmem_limit_bytes=MIB + 4 * split * cap * width),
        name="finish",
    )(*map(in_vmem, (*own, *others)))


def solution(mesh):
    in_specs = (
        P("tenant", None, None),
        P("tenant"),
        P("tenant"),
        P("tenant", None),
        P("tenant", None, "tp"),
        P("tenant", None, "tp"),
        P("tenant", None, "tp"),
        P("tenant", "tp", None),
        P("tenant", None, "tp"),
    )
    out_specs = P(("tenant", "tp"), None)
    tenants = mesh.shape["tenant"]

    def body(*args):
        return per_device(tenants, mesh.shape["tp"], *args)

    return jax.shard_map(
        body, mesh=mesh, in_specs=in_specs, out_specs=out_specs, check_vma=False
    )
```

```python
import functools
import math

import jax
import jax.numpy as jnp
import numpy as np
from jax import lax
from jax.experimental import pallas as pl
from jax.experimental.pallas import tpu as pltpu
from jax.sharding import PartitionSpec as P


LANES = 128
SEG_ROWS = 8
BLOCK = 256
MASKED = -1000000000.0
VMEM = pl.BlockSpec(memory_space=pltpu.VMEM)
SMEM = pl.BlockSpec(memory_space=pltpu.SMEM)
HBM = pl.BlockSpec(memory_space=pltpu.HBM)
MIB = 2**20


def in_vmem(value):
    return pltpu.with_memory_space_constraint(value, pltpu.VMEM)


def in_hbm(value):
    return pltpu.with_memory_space_constraint(value, pltpu.HBM)


def bucket_of(distance, buckets):
    half_count = buckets // 2
    exact_limit = half_count // 2
    size = abs(distance)
    if size < exact_limit:
        found = size
    else:
        found = exact_limit + int(
            np.floor(
                np.log(size / exact_limit)
                / math.log(128.0 / exact_limit)
                * (half_count - exact_limit)
            )
        )
        found = min(found, half_count - 1)
    return found + (half_count if distance > 0 else 0)


def bias_runs(extent, buckets):
    runs = []
    for distance in range(-extent + 1, extent):
        bucket = bucket_of(distance, buckets)
        if not runs or runs[-1][1] != bucket:
            runs.append((distance, bucket))
    return runs


def plan(tenants):
    half, split = tenants // 2, tenants // 4
    near = []
    for i in range(split - 1):
        near.append(((half - 1 - i, half - 1 - i - split),) * 2)
    near.append(((split, split),) * 2)
    far = []
    for i in range(0, split, 2):
        top = tenants - 1 - i
        far.append(((top, top - split), (top - 1, top - 1 - split)))
    return near, far


def halved(pair):
    return pair[0] == pair[1] != 0


def pick(outer, core, table):
    rows = [
        row[0] if row[0] == row[1] else jnp.where(core == 0, row[0], row[1]) for row in table
    ]
    return jnp.int32(rows[0] if table[0] == table[1] else jnp.where(outer == 0, *rows))


def pack_kernel(rounds, cap, runs, tenant_hbm, length_hbm, table_hbm, tokens_hbm, *refs):
    out_refs, strip_ref = refs[:-7], refs[-7]
    select, tokens_ref, tenant_ref, length_ref, table_ref, semaphore = refs[-6:]
    pairs = tenant_ref.shape[0]
    columns = tokens_ref.shape[1]
    tables = [
        pltpu.make_async_copy(tenant_hbm, tenant_ref, semaphore.at[0]),
        pltpu.make_async_copy(length_hbm, length_ref, semaphore.at[1]),
        pltpu.make_async_copy(table_hbm, table_ref, semaphore.at[2]),
    ]
    for copy in tables:
        copy.start()
    step = columns // 2
    fetches = []
    for i, at in enumerate(range(0, columns, step)):
        where = slice(at, at + step)
        fetches.append(
            pltpu.make_async_copy(
                tokens_hbm.at[:, where], tokens_ref.at[:, where], semaphore.at[3 + i]
            )
        )
        fetches[-1].start()
    for copy in tables:
        copy.wait()
    me = lax.axis_index("tenant")
    outer, core = lax.axis_index("tp") // 2, lax.rem(lax.axis_index("tp"), 2)
    side = LANES // cap
    lane = lax.broadcasted_iota(jnp.int32, (1, LANES), 1)
    place = lax.rem(lane, cap)
    part = lane // cap
    rows = lax.broadcasted_iota(jnp.int32, (cap, LANES), 0)
    for slot, table in enumerate(rounds):
        bound = lax.bitwise_xor(me, pick(outer, core, table))
        offset = jnp.int32(0)
        seg = jnp.full((1, LANES), -1, jnp.int32)
        for group in range(pairs // side):
            first = jnp.zeros((1, LANES), jnp.int32)
            last = jnp.zeros((1, LANES), jnp.int32)
            for k in range(side):
                j = group * side + k
                live = jnp.where(tenant_ref[j] == bound, length_ref[j], 0)
                seg = jnp.where((place >= offset) & (place < offset + live), j, seg)
                first = jnp.where(part == k, offset, first)
                last = jnp.where(part == k, live, last)
                offset = offset + live
            target = jnp.where(place < last, first + place, -1)
            select[slot * cap : (slot + 1) * cap, group * LANES : (group + 1) * LANES] = (
                jnp.where(rows == target, 1.0, 0.0).astype(jnp.bfloat16)
            )
        out_refs[slot][out_refs[slot].shape[0] - SEG_ROWS :, :] = jnp.broadcast_to(
            seg.astype(jnp.float32), (SEG_ROWS, LANES)
        ).astype(jnp.bfloat16)
    heads, band, double = strip_ref.shape
    distance = (
        lax.broadcasted_iota(jnp.int32, (band, double), 1)
        - lax.broadcasted_iota(jnp.int32, (band, double), 0)
        - double // 2
    )
    for head in range(heads):
        strip = jnp.full(distance.shape, table_ref[head, runs[0][1]], jnp.float32)
        for start, bucket in runs[1:]:
            strip = jnp.where(distance >= start, table_ref[head, bucket], strip)
        strip_ref[head] = strip
    for fetch, at in zip(fetches, range(0, columns, step)):
        fetch.wait()
        packed = jnp.dot(
            select[...], tokens_ref[:, at : at + step], preferred_element_type=jnp.float32
        ).astype(jnp.bfloat16)
        for slot, out_ref in enumerate(out_refs):
            part = out_ref.shape[0] < columns // LANES * cap

            def store(first, slot=slot, out_ref=out_ref, packed=packed):
                for c in range(step // LANES):
                    out_ref[(first + c) * cap : (first + c + 1) * cap, :] = packed[
                        slot * cap : (slot + 1) * cap, c * LANES : (c + 1) * LANES
                    ]

            if part:
                pl.when(core == at // step)(functools.partial(store, 0))
            else:
                store(at // LANES)


def bias_kernel(strip_ref, bias_ref):
    heads, band, double = strip_ref.shape
    extent = double // 2
    for head in range(heads):
        strip = strip_ref[head]
        for row in range(0, extent, band):
            turned = pltpu.roll(strip, (row - extent) % double, 1)
            bias_ref[head, row : row + band] = turned[:, :extent]


def project_kernel(slots, half, cap, *refs):
    split = half // 2
    slot_refs = refs[: len(slots)]
    gain_ref, wq_ref, wk_ref, wv_ref, x, seg, q, k, v, normed = refs[len(slots) :]
    width = x.shape[1]
    count = seg.shape[0]
    part = count // 2
    me = lax.axis_index("tenant")
    core = lax.rem(lax.axis_index("tp"), 2)

    def place(ref, at, first):
        for c in range((ref.shape[0] - SEG_ROWS) // cap):
            x[
                pl.ds(pl.multiple_of(at * cap, cap), cap),
                (first + c) * LANES : (first + c + 1) * LANES,
            ] = ref[c * cap : (c + 1) * cap, :]

    for ref, (pair, source) in zip(slot_refs, slots):
        mine = lax.rem(lax.bitwise_xor(me, pick(0, core, (pair, pair))) // split, 2) == core
        at = jnp.where(mine, part, 0) + (pair[0] % part)
        if source is None:
            place(ref, at, 0)
        else:
            for side in (0, 1):
                pl.when(core == (side ^ source))(
                    functools.partial(place, ref, at, side * (width // LANES // 2))
                )
        seg[at] = ref[ref.shape[0] - SEG_ROWS :, :].astype(jnp.float32)
    total = count * cap
    step = min(BLOCK, total)
    for base in range(0, total, step):
        rows = slice(base, base + step)
        values = x[rows].astype(jnp.float32)
        mean_square = jnp.mean(values * values, axis=-1, keepdims=True)
        normed[...] = (values * lax.rsqrt(mean_square + 1e-06) * gain_ref[...]).astype(
            jnp.bfloat16
        )
        for w_ref, out in ((wq_ref, q), (wk_ref, k), (wv_ref, v)):
            out[rows] = jnp.dot(
                normed[...], w_ref[...], preferred_element_type=jnp.float32
            ).astype(jnp.bfloat16)


def attend_kernel(far, half, cap, *refs):
    x, seg, q, k, v, wo_ref, bias_ref, send_ref, keep_ref, context, score, top, weight = refs
    count = seg.shape[0]
    part = count // 2
    me = lax.axis_index("tenant")
    outer = lax.axis_index("tp") // 2
    total = count * cap
    step = min(BLOCK, total)
    inner = min(LANES, total)
    side = inner // cap
    heads = bias_ref.shape[0]
    size = q.shape[1] // heads
    lane = lax.broadcasted_iota(jnp.int32, (1, inner), 1)
    diagonal = lax.broadcasted_iota(jnp.int32, (inner, inner), 0) == lax.broadcasted_iota(
        jnp.int32, (inner, inner), 1
    )
    owner = (me // half == outer) if not far else (me // half != outer)
    ones = jnp.ones((inner, size), jnp.bfloat16)
    scale = jnp.where(owner, 1.0, 0.0).astype(jnp.float32)
    for base in range(0, total, step):
        blocks = step // inner
        for block in range(blocks):
            first = (base + block * inner) // cap
            code = jnp.full((1, inner), -1.0, jnp.float32)
            for s in range(side):
                one = seg[first + s][:1, :inner]
                one = jnp.where(one >= 0.0, one + 1024.0 * s, -1.0)
                code = jnp.where(lane // cap == s, one, code)
            down = jnp.sum(jnp.where(diagonal, code, 0.0), axis=1, keepdims=True)
            allowed = down == jnp.where(code >= 0.0, code, -2.0)
            alive = jnp.broadcast_to(down >= 0.0, (inner, inner))
            at = slice(block * inner, (block + 1) * inner)
            row = slice(base + at.start, base + at.stop)
            for head in range(heads):
                cols = slice(head * size, (head + 1) * size)
                scores = lax.dot_general(
                    q[row, cols],
                    k[row, cols],
                    (((1,), (1,)), ((), ())),
                    preferred_element_type=jnp.float32,
                )
                scores = jnp.where(allowed, scores + bias_ref[head], MASKED)
                score[head] = scores
                top[head] = jnp.broadcast_to(
                    jnp.max(scores, axis=-1, keepdims=True), (inner, inner)
                )
            for head in range(heads):
                weight[head] = jnp.exp(score[head] - top[head]).astype(jnp.bfloat16)
            for head in range(heads):
                cols = slice(head * size, (head + 1) * size)
                both = jnp.dot(
                    weight[head],
                    jnp.concatenate([v[row, cols], ones], axis=1),
                    preferred_element_type=jnp.float32,
                )
                context[at, cols] = jnp.where(
                    alive, both[:, :size] * (1.0 / both[:, size:]), 0.0
                ).astype(jnp.bfloat16)
        partial = jnp.dot(context[...], wo_ref[...], preferred_element_type=jnp.float32)
        size_out = min(step, part * cap)
        for at in range(0, step, size_out):
            row = base + at
            piece = partial[at : at + size_out]
            if row < part * cap:
                send_ref[row : row + size_out] = piece.astype(jnp.bfloat16)
            else:
                keep_ref[row - part * cap : row - part * cap + size_out] = (
                    piece + scale * x[row : row + size_out].astype(jnp.float32)
                )


def sublayer_kernel(slots, far, half, cap, *refs):
    count = len(slots)
    inputs, (gain_ref, wq_ref, wk_ref, wv_ref, wo_ref, bias_ref, send_ref, keep_ref) = (
        refs[:count],
        refs[count : count + 8],
    )
    x, seg, normed, q, k, v, context, score, top, weight = refs[count + 8 :]
    project_kernel(
        slots, half, cap, *inputs, gain_ref, wq_ref, wk_ref, wv_ref, x, seg, q, k, v, normed
    )
    attend_kernel(
        far, half, cap, x, seg, q, k, v, wo_ref, bias_ref, send_ref, keep_ref, context, score, top, weight
    )


def join_kernel(turn, near_keep, near_got, far_keep, far_got, own_ref, send_ref):
    cap = far_keep.shape[0]
    split = near_keep.shape[0] // cap
    outer = lax.axis_index("tp") // 2
    half = lax.axis_size("tenant") // 2
    owner = lax.axis_index("tenant") // half == outer
    first, later = turn
    relative = split - 1 - first - lax.rem(outer + later, 2)
    rows = pl.ds(pl.multiple_of(relative * cap, cap), cap)
    near = near_keep[rows, :] + near_got[rows, :].astype(jnp.float32)
    far = far_keep[...] + far_got[...].astype(jnp.float32)
    own_ref[...] = jnp.where(owner, near, far)
    send_ref[...] = jnp.where(owner, far, near).astype(jnp.bfloat16)


def finish_kernel(cap, *refs):
    pieces = len(refs) // 2
    own_refs, other_refs, out_ref = refs[:pieces], refs[pieces:-1], refs[-1]
    me = lax.axis_index("tenant")
    outer = lax.axis_index("tp") // 2
    direct = pieces // 2
    for i in range(pieces):
        pair = 2 * (i % direct) + lax.rem(outer + i // direct, 2)
        at = lax.bitwise_xor(lax.rem(me, pieces), pieces - 1 - pair)
        out_ref[pl.ds(pl.multiple_of(at * cap, cap), cap), :] = (
            own_refs[i][...] + other_refs[(i + direct) % pieces][...].astype(jnp.float32)
        ).astype(jnp.bfloat16)


def per_device(
    tenants,
    tp,
    src_tokens,
    pair_tenant,
    pair_length,
    norm_gain,
    w_query,
    w_key,
    w_value,
    w_out,
    rel_bias,
):
    pairs, cap, width = src_tokens.shape
    half, split = tenants // 2, tenants // 4
    near, far = plan(tenants)
    rounds = near + far + [((0, 0),) * 2]
    slot_shapes = [
        pltpu.VMEM(
            (width // LANES * cap // (2 if halved(table[0]) else 1) + SEG_ROWS, LANES),
            jnp.bfloat16,
        )
        for table in rounds
    ]
    buckets, heads = rel_bias.shape[1:]
    extent = min(LANES, half * cap)
    *packed, strips = pl.pallas_call(
        functools.partial(pack_kernel, rounds, cap, bias_runs(extent, buckets)),
        out_shape=slot_shapes
        + [pltpu.VMEM((heads, 8, 2 * extent), jnp.float32)],
        in_specs=[HBM] * 4,
        out_specs=[VMEM] * (len(rounds) + 1),
        scratch_shapes=[
            pltpu.VMEM((len(rounds) * cap, pairs * cap), jnp.bfloat16),
            pltpu.VMEM((pairs * cap, width), jnp.bfloat16),
            pltpu.SMEM((pairs,), jnp.int32),
            pltpu.SMEM((pairs,), jnp.int32),
            pltpu.SMEM((heads, buckets), jnp.float32),
            pltpu.SemaphoreType.DMA((5,)),
        ],
        compiler_params=pltpu.CompilerParams(
            vmem_limit_bytes=2 * MIB + 2 * pairs * cap * (width + (len(rounds) + 1) * cap)
        ),
        name="pack",
    )(
        *map(
            in_hbm,
            (
                pair_tenant,
                pair_length,
                rel_bias[0].T,
                src_tokens.reshape(pairs * cap, width),
            ),
        )
    )

    def shift(value, table):
        moves = []
        for u in range(tenants):
            for t in range(tp):
                moves.append((u * tp + t, (u ^ table[t // 2][t % 2]) * tp + t))
        return lax.ppermute(value, ("tenant", "tp"), moves)

    def swap(value):
        return lax.ppermute(value, "tp", [(t, t ^ 1) for t in range(tp)])

    def trade(value):
        return lax.ppermute(value, "tp", [(t, t ^ 2) for t in range(tp)])

    arrived = []
    for value, table in zip(packed, rounds[:-1]):
        arrived.append(shift(value, table))

    weights = [w[0] for w in (w_query, w_key, w_value, w_out)]
    bias = pl.pallas_call(
        bias_kernel,
        out_shape=pltpu.VMEM((heads, extent, extent), jnp.float32),
        in_specs=[VMEM],
        out_specs=VMEM,
        compiler_params=pltpu.CompilerParams(vmem_limit_bytes=4 * MIB),
        cost_estimate=pl.CostEstimate(
            flops=10**10, bytes_accessed=0, transcendentals=0
        ),
        name="prepare",
    )(in_vmem(strips))

    def sublayer(rounds_here, values, is_far):
        slots, arrays = [], []
        for pair, value in zip(rounds_here, values):
            slots.append((pair, 0 if halved(pair) else None))
            arrays.append(value)
            if pair != (0, 0):
                slots.append((pair[::-1], 1 if halved(pair) else None))
                arrays.append(swap(value))
        count = 2 * len(rounds_here) if is_far else half
        total = count * cap
        step = min(BLOCK, total)
        inner = min(LANES, total)
        own = w_query.shape[2]
        params = pltpu.CompilerParams(vmem_limit_bytes=8 * MIB + 10 * total * width)
        sums = [
            pltpu.VMEM((total // 2, width), jnp.bfloat16),
            pltpu.VMEM((total // 2, width), jnp.float32),
        ]
        rows = [
            pltpu.VMEM((total, width), jnp.bfloat16),
            pltpu.VMEM((count, SEG_ROWS, LANES), jnp.float32),
        ]
        projected = [pltpu.VMEM((total, own), jnp.bfloat16)] * 3
        normed = [pltpu.VMEM((step, width), jnp.bfloat16)]
        scratch = [
            pltpu.VMEM((step, own), jnp.bfloat16),
            pltpu.VMEM((heads, inner, inner), jnp.float32),
            pltpu.VMEM((heads, inner, inner), jnp.float32),
            pltpu.VMEM((heads, inner, inner), jnp.bfloat16),
        ]
        first = (*map(in_vmem, arrays), norm_gain, *map(in_vmem, weights[:3]))
        last = (in_vmem(weights[3]), in_vmem(bias))
        send, keep = pl.pallas_call(
            functools.partial(sublayer_kernel, slots, is_far, half, cap),
            out_shape=sums,
            in_specs=[VMEM] * (len(slots) + 6),
            out_specs=[VMEM] * 2,
            scratch_shapes=rows + normed + projected + scratch,
            compiler_params=params,
        )(*first, *last)
        return keep, swap(send)

    shifts = [table[0] for table in near] + [(0, 0)]
    near_sums = sublayer(shifts, arrived[: len(near)] + [packed[-1]], False)
    direct = arrived[len(near) :]
    traded = []
    for value in direct:
        traded.append(trade(value))
    own, others = [], []
    for i, value in enumerate(direct + traded):
        later, k = divmod(i, len(direct))
        far_sums = sublayer([far[k][0]], [value], True)
        kept, send = pl.pallas_call(
            functools.partial(join_kernel, (2 * k, later)),
            out_shape=[
                pltpu.VMEM((cap, width), jnp.float32),
                pltpu.VMEM((cap, width), jnp.bfloat16),
            ],
            in_specs=[VMEM] * 4,
            out_specs=[VMEM] * 2,
            compiler_params=pltpu.CompilerParams(vmem_limit_bytes=MIB),
        )(*map(in_vmem, (*near_sums, *far_sums)))
        others.append(trade(send))
        own.append(kept)
    return pl.pallas_call(
        functools.partial(finish_kernel, cap),
        out_shape=jax.ShapeDtypeStruct((split * cap, width), jnp.bfloat16),
        in_specs=[VMEM] * (2 * split),
        out_specs=VMEM,
        compiler_params=pltpu.CompilerParams(vmem_limit_bytes=MIB + 4 * split * cap * width),
        name="finish",
    )(*map(in_vmem, (*own, *others)))


def solution(mesh):
    in_specs = (
        P("tenant", None, None),
        P("tenant"),
        P("tenant"),
        P("tenant", None),
        P("tenant", None, "tp"),
        P("tenant", None, "tp"),
        P("tenant", None, "tp"),
        P("tenant", "tp", None),
        P("tenant", None, "tp"),
    )
    out_specs = P(("tenant", "tp"), None)
    tenants = mesh.shape["tenant"]

    def body(*args):
        return per_device(tenants, mesh.shape["tp"], *args)

    return jax.shard_map(
        body, mesh=mesh, in_specs=in_specs, out_specs=out_specs, check_vma=False
    )
```

```python
import functools
import math

import jax
import jax.numpy as jnp
import numpy as np
from jax import lax
from jax.experimental import pallas as pl
from jax.experimental.pallas import tpu as pltpu
from jax.sharding import PartitionSpec as P


LANES = 128
SEG_ROWS = 8
BLOCK = 256
MASKED = -1000000000.0
VMEM = pl.BlockSpec(memory_space=pltpu.VMEM)
SMEM = pl.BlockSpec(memory_space=pltpu.SMEM)
HBM = pl.BlockSpec(memory_space=pltpu.HBM)
MIB = 2**20


def in_vmem(value):
    return pltpu.with_memory_space_constraint(value, pltpu.VMEM)


def in_hbm(value):
    return pltpu.with_memory_space_constraint(value, pltpu.HBM)


def bucket_of(distance, buckets):
    half_count = buckets // 2
    exact_limit = half_count // 2
    size = abs(distance)
    if size < exact_limit:
        found = size
    else:
        found = exact_limit + int(
            np.floor(
                np.log(size / exact_limit)
                / math.log(128.0 / exact_limit)
                * (half_count - exact_limit)
            )
        )
        found = min(found, half_count - 1)
    return found + (half_count if distance > 0 else 0)


def bias_runs(extent, buckets):
    runs = []
    for distance in range(-extent + 1, extent):
        bucket = bucket_of(distance, buckets)
        if not runs or runs[-1][1] != bucket:
            runs.append((distance, bucket))
    return runs


def plan(tenants):
    half, split = tenants // 2, tenants // 4
    near = []
    for i in range(split - 1):
        near.append(((half - 1 - i, half - 1 - i - split),) * 2)
    near.append(((split, split),) * 2)
    far = []
    for i in range(0, split, 2):
        top = tenants - 1 - i
        far.append(((top, top - split), (top - 1, top - 1 - split)))
    return near, far


def halved(pair):
    return pair[0] == pair[1] != 0


def pick(outer, core, table):
    rows = [
        row[0] if row[0] == row[1] else jnp.where(core == 0, row[0], row[1]) for row in table
    ]
    return jnp.int32(rows[0] if table[0] == table[1] else jnp.where(outer == 0, *rows))


def pack_kernel(rounds, cap, runs, tenant_hbm, length_hbm, table_hbm, tokens_hbm, *refs):
    out_refs, strip_ref = refs[:-7], refs[-7]
    select, tokens_ref, tenant_ref, length_ref, table_ref, semaphore = refs[-6:]
    pairs = tenant_ref.shape[0]
    columns = tokens_ref.shape[1]
    tables = [
        pltpu.make_async_copy(tenant_hbm, tenant_ref, semaphore.at[0]),
        pltpu.make_async_copy(length_hbm, length_ref, semaphore.at[1]),
        pltpu.make_async_copy(table_hbm, table_ref, semaphore.at[2]),
    ]
    for copy in tables:
        copy.start()
    step = columns // 2
    fetches = []
    for i, at in enumerate(range(0, columns, step)):
        where = slice(at, at + step)
        fetches.append(
            pltpu.make_async_copy(
                tokens_hbm.at[:, where], tokens_ref.at[:, where], semaphore.at[3 + i]
            )
        )
        fetches[-1].start()
    for copy in tables:
        copy.wait()
    me = lax.axis_index("tenant")
    outer, core = lax.axis_index("tp") // 2, lax.rem(lax.axis_index("tp"), 2)
    side = LANES // cap
    lane = lax.broadcasted_iota(jnp.int32, (1, LANES), 1)
    place = lax.rem(lane, cap)
    part = lane // cap
    rows = lax.broadcasted_iota(jnp.int32, (cap, LANES), 0)
    for slot, table in enumerate(rounds):
        bound = lax.bitwise_xor(me, pick(outer, core, table))
        offset = jnp.int32(0)
        seg = jnp.full((1, LANES), -1, jnp.int32)
        for group in range(pairs // side):
            first = jnp.zeros((1, LANES), jnp.int32)
            last = jnp.zeros((1, LANES), jnp.int32)
            for k in range(side):
                j = group * side + k
                live = jnp.where(tenant_ref[j] == bound, length_ref[j], 0)
                seg = jnp.where((place >= offset) & (place < offset + live), j, seg)
                first = jnp.where(part == k, offset, first)
                last = jnp.where(part == k, live, last)
                offset = offset + live
            target = jnp.where(place < last, first + place, -1)
            select[slot * cap : (slot + 1) * cap, group * LANES : (group + 1) * LANES] = (
                jnp.where(rows == target, 1.0, 0.0).astype(jnp.bfloat16)
            )
        out_refs[slot][out_refs[slot].shape[0] - SEG_ROWS :, :] = jnp.broadcast_to(
            seg.astype(jnp.float32), (SEG_ROWS, LANES)
        ).astype(jnp.bfloat16)
    heads, band, double = strip_ref.shape
    distance = (
        lax.broadcasted_iota(jnp.int32, (band, double), 1)
        - lax.broadcasted_iota(jnp.int32, (band, double), 0)
        - double // 2
    )
    for head in range(heads):
        strip = jnp.full(distance.shape, table_ref[head, runs[0][1]], jnp.float32)
        for start, bucket in runs[1:]:
            strip = jnp.where(distance >= start, table_ref[head, bucket], strip)
        strip_ref[head] = strip
    for fetch, at in zip(fetches, range(0, columns, step)):
        fetch.wait()
        packed = jnp.dot(
            select[...], tokens_ref[:, at : at + step], preferred_element_type=jnp.float32
        ).astype(jnp.bfloat16)
        for slot, out_ref in enumerate(out_refs):
            part = out_ref.shape[0] < columns // LANES * cap

            def store(first, slot=slot, out_ref=out_ref, packed=packed):
                for c in range(step // LANES):
                    out_ref[(first + c) * cap : (first + c + 1) * cap, :] = packed[
                        slot * cap : (slot + 1) * cap, c * LANES : (c + 1) * LANES
                    ]

            if part:
                pl.when(core == at // step)(functools.partial(store, 0))
            else:
                store(at // LANES)


def bias_kernel(strip_ref, bias_ref):
    heads, band, double = strip_ref.shape
    extent = double // 2
    for head in range(heads):
        strip = strip_ref[head]
        for row in range(0, extent, band):
            turned = pltpu.roll(strip, (row - extent) % double, 1)
            bias_ref[head, row : row + band] = turned[:, :extent]


def project_kernel(slots, half, cap, *refs):
    split = half // 2
    slot_refs = refs[: len(slots)]
    gain_ref, wq_ref, wk_ref, wv_ref, x, seg, q, k, v, normed = refs[len(slots) :]
    width = x.shape[1]
    count = seg.shape[0]
    part = count // 2
    me = lax.axis_index("tenant")
    core = lax.rem(lax.axis_index("tp"), 2)

    def place(ref, at, first):
        for c in range((ref.shape[0] - SEG_ROWS) // cap):
            x[
                pl.ds(pl.multiple_of(at * cap, cap), cap),
                (first + c) * LANES : (first + c + 1) * LANES,
            ] = ref[c * cap : (c + 1) * cap, :]

    for ref, (pair, source) in zip(slot_refs, slots):
        mine = lax.rem(lax.bitwise_xor(me, pick(0, core, (pair, pair))) // split, 2) == core
        at = jnp.where(mine, part, 0) + (pair[0] % part)
        if source is None:
            place(ref, at, 0)
        else:
            for side in (0, 1):
                pl.when(core == (side ^ source))(
                    functools.partial(place, ref, at, side * (width // LANES // 2))
                )
        seg[at] = ref[ref.shape[0] - SEG_ROWS :, :].astype(jnp.float32)
    total = count * cap
    step = min(BLOCK, total)
    for base in range(0, total, step):
        rows = slice(base, base + step)
        values = x[rows].astype(jnp.float32)
        mean_square = jnp.mean(values * values, axis=-1, keepdims=True)
        normed[...] = (values * lax.rsqrt(mean_square + 1e-06) * gain_ref[...]).astype(
            jnp.bfloat16
        )
        for w_ref, out in ((wq_ref, q), (wk_ref, k), (wv_ref, v)):
            out[rows] = jnp.dot(
                normed[...], w_ref[...], preferred_element_type=jnp.float32
            ).astype(jnp.bfloat16)


def attend_kernel(far, half, cap, *refs):
    x, seg, q, k, v, wo_ref, bias_ref, send_ref, keep_ref, context, score, top, weight = refs
    count = seg.shape[0]
    part = count // 2
    me = lax.axis_index("tenant")
    outer = lax.axis_index("tp") // 2
    total = count * cap
    step = min(BLOCK, total)
    inner = min(LANES, total)
    side = inner // cap
    heads = bias_ref.shape[0]
    size = q.shape[1] // heads
    lane = lax.broadcasted_iota(jnp.int32, (1, inner), 1)
    diagonal = lax.broadcasted_iota(jnp.int32, (inner, inner), 0) == lax.broadcasted_iota(
        jnp.int32, (inner, inner), 1
    )
    owner = (me // half == outer) if not far else (me // half != outer)
    ones = jnp.ones((inner, size), jnp.bfloat16)
    scale = jnp.where(owner, 1.0, 0.0).astype(jnp.float32)
    for base in range(0, total, step):
        blocks = step // inner
        for block in range(blocks):
            first = (base + block * inner) // cap
            code = jnp.full((1, inner), -1.0, jnp.float32)
            for s in range(side):
                one = seg[first + s][:1, :inner]
                one = jnp.where(one >= 0.0, one + 1024.0 * s, -1.0)
                code = jnp.where(lane // cap == s, one, code)
            down = jnp.sum(jnp.where(diagonal, code, 0.0), axis=1, keepdims=True)
            allowed = down == jnp.where(code >= 0.0, code, -2.0)
            alive = jnp.broadcast_to(down >= 0.0, (inner, inner))
            at = slice(block * inner, (block + 1) * inner)
            row = slice(base + at.start, base + at.stop)
            for head in range(heads):
                cols = slice(head * size, (head + 1) * size)
                scores = lax.dot_general(
                    q[row, cols],
                    k[row, cols],
                    (((1,), (1,)), ((), ())),
                    preferred_element_type=jnp.float32,
                )
                scores = jnp.where(allowed, scores + bias_ref[head], MASKED)
                score[head] = scores
                top[head] = jnp.broadcast_to(
                    jnp.max(scores, axis=-1, keepdims=True), (inner, inner)
                )
            for head in range(heads):
                weight[head] = jnp.exp(score[head] - top[head]).astype(jnp.bfloat16)
            for head in range(heads):
                cols = slice(head * size, (head + 1) * size)
                both = jnp.dot(
                    weight[head],
                    jnp.concatenate([v[row, cols], ones], axis=1),
                    preferred_element_type=jnp.float32,
                )
                context[at, cols] = jnp.where(
                    alive, both[:, :size] * (1.0 / both[:, size:]), 0.0
                ).astype(jnp.bfloat16)
        partial = jnp.dot(context[...], wo_ref[...], preferred_element_type=jnp.float32)
        size_out = min(step, part * cap)
        for at in range(0, step, size_out):
            row = base + at
            piece = partial[at : at + size_out]
            if row < part * cap:
                send_ref[row : row + size_out] = piece.astype(jnp.bfloat16)
            else:
                keep_ref[row - part * cap : row - part * cap + size_out] = (
                    piece + scale * x[row : row + size_out].astype(jnp.float32)
                )


def sublayer_kernel(slots, far, half, cap, *refs):
    count = len(slots)
    inputs, (gain_ref, wq_ref, wk_ref, wv_ref, wo_ref, bias_ref, send_ref, keep_ref) = (
        refs[:count],
        refs[count : count + 8],
    )
    x, seg, normed, q, k, v, context, score, top, weight = refs[count + 8 :]
    project_kernel(
        slots, half, cap, *inputs, gain_ref, wq_ref, wk_ref, wv_ref, x, seg, q, k, v, normed
    )
    attend_kernel(
        far, half, cap, x, seg, q, k, v, wo_ref, bias_ref, send_ref, keep_ref, context, score, top, weight
    )


def join_kernel(turn, near_keep, near_got, far_keep, far_got, own_ref, send_ref):
    cap = far_keep.shape[0]
    split = near_keep.shape[0] // cap
    outer = lax.axis_index("tp") // 2
    half = lax.axis_size("tenant") // 2
    owner = lax.axis_index("tenant") // half == outer
    first, later = turn
    relative = split - 1 - first - lax.rem(outer + later, 2)
    rows = pl.ds(pl.multiple_of(relative * cap, cap), cap)
    near = near_keep[rows, :] + near_got[rows, :].astype(jnp.float32)
    far = far_keep[...] + far_got[...].astype(jnp.float32)
    own_ref[...] = jnp.where(owner, near, far)
    send_ref[...] = jnp.where(owner, far, near).astype(jnp.bfloat16)


def finish_kernel(cap, *refs):
    pieces = len(refs) // 2
    own_refs, other_refs, out_ref = refs[:pieces], refs[pieces:-1], refs[-1]
    me = lax.axis_index("tenant")
    outer = lax.axis_index("tp") // 2
    direct = pieces // 2
    for i in range(pieces):
        pair = 2 * (i % direct) + lax.rem(outer + i // direct, 2)
        at = lax.bitwise_xor(lax.rem(me, pieces), pieces - 1 - pair)
        out_ref[pl.ds(pl.multiple_of(at * cap, cap), cap), :] = (
            own_refs[i][...] + other_refs[(i + direct) % pieces][...].astype(jnp.float32)
        ).astype(jnp.bfloat16)


def per_device(
    tenants,
    tp,
    src_tokens,
    pair_tenant,
    pair_length,
    norm_gain,
    w_query,
    w_key,
    w_value,
    w_out,
    rel_bias,
):
    pairs, cap, width = src_tokens.shape
    half, split = tenants // 2, tenants // 4
    near, far = plan(tenants)
    rounds = near + far + [((0, 0),) * 2]
    slot_shapes = [
        pltpu.VMEM(
            (width // LANES * cap // (2 if halved(table[0]) else 1) + SEG_ROWS, LANES),
            jnp.bfloat16,
        )
        for table in rounds
    ]
    buckets, heads = rel_bias.shape[1:]
    extent = min(LANES, half * cap)
    *packed, strips = pl.pallas_call(
        functools.partial(pack_kernel, rounds, cap, bias_runs(extent, buckets)),
        out_shape=slot_shapes
        + [pltpu.VMEM((heads, 8, 2 * extent), jnp.float32)],
        in_specs=[HBM] * 4,
        out_specs=[VMEM] * (len(rounds) + 1),
        scratch_shapes=[
            pltpu.VMEM((len(rounds) * cap, pairs * cap), jnp.bfloat16),
            pltpu.VMEM((pairs * cap, width), jnp.bfloat16),
            pltpu.SMEM((pairs,), jnp.int32),
            pltpu.SMEM((pairs,), jnp.int32),
            pltpu.SMEM((heads, buckets), jnp.float32),
            pltpu.SemaphoreType.DMA((5,)),
        ],
        compiler_params=pltpu.CompilerParams(
            vmem_limit_bytes=2 * MIB + 2 * pairs * cap * (width + (len(rounds) + 1) * cap)
        ),
        name="pack",
    )(
        *map(
            in_hbm,
            (
                pair_tenant,
                pair_length,
                rel_bias[0].T,
                src_tokens.reshape(pairs * cap, width),
            ),
        )
    )

    def shift(value, table):
        moves = []
        for u in range(tenants):
            for t in range(tp):
                moves.append((u * tp + t, (u ^ table[t // 2][t % 2]) * tp + t))
        return lax.ppermute(value, ("tenant", "tp"), moves)

    def swap(value):
        return lax.ppermute(value, "tp", [(t, t ^ 1) for t in range(tp)])

    def trade(value):
        return lax.ppermute(value, "tp", [(t, t ^ 2) for t in range(tp)])

    arrived = []
    for value, table in zip(packed, rounds[:-1]):
        arrived.append(shift(value, table))

    weights = [w[0] for w in (w_query, w_key, w_value, w_out)]
    bias = pl.pallas_call(
        bias_kernel,
        out_shape=pltpu.VMEM((heads, extent, extent), jnp.float32),
        in_specs=[VMEM],
        out_specs=VMEM,
        compiler_params=pltpu.CompilerParams(vmem_limit_bytes=4 * MIB),
        cost_estimate=pl.CostEstimate(
            flops=10**10, bytes_accessed=0, transcendentals=0
        ),
        name="prepare",
    )(in_vmem(strips))

    def sublayer(rounds_here, values, is_far, parts):
        slots, arrays = [], []
        for pair, value in zip(rounds_here, values):
            slots.append((pair, 0 if halved(pair) else None))
            arrays.append(value)
            if pair != (0, 0):
                slots.append((pair[::-1], 1 if halved(pair) else None))
                arrays.append(swap(value))
        count = 2 * len(rounds_here) if is_far else half
        total = count * cap
        step = min(BLOCK, total)
        inner = min(LANES, total)
        own = w_query.shape[2]
        params = pltpu.CompilerParams(
            vmem_limit_bytes=8 * MIB + 10 * total * width)
        sums = [
            pltpu.VMEM((total // 2, width), jnp.bfloat16),
            pltpu.VMEM((total // 2, width), jnp.float32),
        ]
        rows = [
            pltpu.VMEM((total, width), jnp.bfloat16),
            pltpu.VMEM((count, SEG_ROWS, LANES), jnp.float32),
        ]
        projected = [pltpu.VMEM((total, own), jnp.bfloat16)] * 3
        normed = [pltpu.VMEM((step, width), jnp.bfloat16)]
        scratch = [
            pltpu.VMEM((step, own), jnp.bfloat16),
            pltpu.VMEM((heads, inner, inner), jnp.float32),
            pltpu.VMEM((heads, inner, inner), jnp.float32),
            pltpu.VMEM((heads, inner, inner), jnp.bfloat16),
        ]
        first = (*map(in_vmem, arrays), norm_gain, *map(in_vmem, weights[:3]))
        last = (in_vmem(weights[3]), in_vmem(bias))
        if parts == 1:
            send, keep = pl.pallas_call(
                functools.partial(sublayer_kernel, slots, is_far, half, cap),
                out_shape=sums,
                in_specs=[VMEM] * (len(slots) + 6),
                out_specs=[VMEM] * 2,
                scratch_shapes=rows + normed + projected + scratch,
                compiler_params=params,
            )(*first, *last)
        else:
            made = pl.pallas_call(
                functools.partial(project_kernel, slots, half, cap),
                out_shape=rows + projected,
                in_specs=[VMEM] * (len(slots) + 4),
                out_specs=[VMEM] * 5,
                scratch_shapes=normed,
                compiler_params=params,
            )(*first)
            send, keep = pl.pallas_call(
                functools.partial(attend_kernel, is_far, half, cap),
                out_shape=sums,
                in_specs=[VMEM] * 7,
                out_specs=[VMEM] * 2,
                scratch_shapes=scratch,
                compiler_params=params,
            )(*map(in_vmem, made), *last)
        return keep, swap(send)

    shifts = [table[0] for table in near] + [(0, 0)]
    near_sums = sublayer(shifts, arrived[: len(near)] + [packed[-1]], False, 2)
    direct = arrived[len(near) :]
    traded = []
    for value in direct:
        traded.append(trade(value))
    own, others = [], []
    for i, value in enumerate(direct + traded):
        later, k = divmod(i, len(direct))
        far_sums = sublayer([far[k][0]], [value], True, 1)
        kept, send = pl.pallas_call(
            functools.partial(join_kernel, (2 * k, later)),
            out_shape=[
                pltpu.VMEM((cap, width), jnp.float32),
                pltpu.VMEM((cap, width), jnp.bfloat16),
            ],
            in_specs=[VMEM] * 4,
            out_specs=[VMEM] * 2,
            compiler_params=pltpu.CompilerParams(vmem_limit_bytes=MIB),
        )(*map(in_vmem, (*near_sums, *far_sums)))
        others.append(trade(send))
        own.append(kept)
    return pl.pallas_call(
        functools.partial(finish_kernel, cap),
        out_shape=jax.ShapeDtypeStruct((split * cap, width), jnp.bfloat16),
        in_specs=[VMEM] * (2 * split),
        out_specs=VMEM,
        compiler_params=pltpu.CompilerParams(vmem_limit_bytes=MIB + 4 * split * cap * width),
        name="finish",
    )(*map(in_vmem, (*own, *others)))


def solution(mesh):
    in_specs = (
        P("tenant", None, None),
        P("tenant"),
        P("tenant"),
        P("tenant", None),
        P("tenant", None, "tp"),
        P("tenant", None, "tp"),
        P("tenant", None, "tp"),
        P("tenant", "tp", None),
        P("tenant", None, "tp"),
    )
    out_specs = P(("tenant", "tp"), None)
    tenants = mesh.shape["tenant"]

    def body(*args):
        return per_device(tenants, mesh.shape["tp"], *args)

    return jax.shard_map(
        body, mesh=mesh, in_specs=in_specs, out_specs=out_specs, check_vma=False
    )
```
